512 devices in a mesh: grp: 16 (over z, x_hi), blk: 32 (over x_lo, y, core).
Axes of the slice: x: 4 (x_hi: 2, x_lo: 2; x = x_hi * 2 + x_lo), y: 8, z: 8, core: 2. Of those that a mesh axis runs over, the one named last changes fastest.
Arguments:
- ao_ints: bfloat16 [128, 1504, 1504], P('grp', 'blk'), may hold values from -6 to 6
- v_coeff: bfloat16 [1504, 1344], P(None, 'blk'), may hold values from -0.15625 to 0.15625
- batch_start: int32 [16], replicated, may hold values from 0 to 1496, as said below
- owner_map: int32 [32], replicated, may hold values from 0 to 31, each once
Outputs:
- slab: bfloat16 [128, 1344, 1344], P(None, 'blk', 'grp')
The draws below stay inside these ranges and needn't reach their ends.
Inputs may be any that keep to these rules, and one draw needn't show every extreme that they name: `batch_start`: distinct multiples of 8; one entry is 0 and one is 1496. `owner_map`: each block number appears once.
All inputs are finite; a program needn't handle non-finite values.
Results may differ from the reference program's by a relative error of at most 0.0049.
Values may be sent and summed in bfloat16 or wider, within the bound.
No kernel may reach another device: no remote copies, remote signals or barrier semaphores. Data moves between devices by JAX's collectives and lax.ppermute only.
A program may use at most 64 MiB of HBM per device.

```python
import jax
import jax.numpy as jnp
from jax import lax

NAO = 1504
NV = 1344
SB = 8
BW = 42
SIG = 128
NBLKB = 32
N_GRP = 16


def draw_batch_start(key, part):
    slot_count = NAO // SB
    inner = 1 + jax.random.permutation(key, slot_count - 2).astype(jnp.int32)
    ends = jnp.array([0, slot_count - 1], dtype=jnp.int32)
    picked = jnp.concatenate([ends, inner[:N_GRP - 2]])
    shuffle = jax.random.permutation(jax.random.fold_in(key, 7), N_GRP)
    return (picked[shuffle] * SB).astype(jnp.int32)


def steps_of(stream_key, extent, shards, least, high):
    def one(axis_at, parts):
        steps = jax.random.uniform(jax.random.fold_in(jax.random.fold_in(stream_key, 6), axis_at), (parts,), jnp.float32, least / len(shards), high / len(shards))
        return jnp.repeat(jnp.exp(steps), extent[axis_at] // parts).reshape((-1,) + (1,) * (len(extent) - axis_at - 1))

    factor_of = one(*shards[0])
    for cut in shards[1:]:
        factor_of = factor_of * one(*cut)
    return factor_of


def centred(key, shape, deviation, reach, pieces=(), kind=jnp.bfloat16):
    loudness = steps_of(key, shape, pieces, -0.22, 0.18) if pieces else 1.0
    entries = jax.random.normal(key, shape, jnp.float32) * deviation * loudness
    return jnp.minimum(jnp.maximum(entries, -reach), reach).astype(kind)


def setup_inputs(seed: int = 0) -> dict:
    streams_of = jax.random.split(jax.random.key(seed), 5)
    return {
        "ao_ints": centred(streams_of[0], (SIG, NAO, NAO), 1.0, 6.0, ((0, 16), (1, 32))),
        "v_coeff": centred(streams_of[1], (NAO, NV), NAO ** -0.5, 0.15625, ((1, 32),)),
        "batch_start": draw_batch_start(jax.random.fold_in(streams_of[4], 71), 0),
        "owner_map": jax.random.permutation(streams_of[3], NBLKB).astype(jnp.int32),
    }


def reference(ao_ints, v_coeff, batch_start, owner_map):
    def one_row(ints_row):
        half_row = jnp.dot(ints_row, v_coeff, preferred_element_type=jnp.float32).astype(jnp.bfloat16)
        return jnp.dot(half_row.T, v_coeff, preferred_element_type=jnp.float32).astype(jnp.bfloat16)

    third = lax.map(one_row, ao_ints)
    group_ids = jnp.arange(N_GRP, dtype=jnp.int32)
    rank = jnp.sum((batch_start[None, :] < batch_start[:, None]).astype(jnp.int32), axis=1)
    source = jnp.sum(group_ids[None, :] * (rank[None, :] == group_ids[:, None]).astype(jnp.int32), axis=1)
    blocks = third.reshape(N_GRP, SB, NV, NV // BW, BW)
    blocks = jnp.take(blocks, source.astype(jnp.int32), axis=0)
    blocks = jnp.take(blocks, owner_map.astype(jnp.int32), axis=3)
    return blocks.reshape(SIG, NV, NV)
```

```python
import functools

import jax
import jax.numpy as jnp
from jax import lax
from jax.experimental import pallas as pl
from jax.experimental.pallas import tpu as pltpu
from jax.sharding import PartitionSpec as P


BF = jnp.bfloat16
F32 = jnp.float32
NX, NY, NZ, NC = 2, 8, 8, 2
XN = 4


def blk_of(xl, y, c):
    return (xl * NY + y) * NC + c


def y_groups():
    return [[blk_of(xl, y, c) for y in range(NY)] for xl in range(NX) for c in range(NC)]


def xy_groups():
    return [[blk_of(xl, y, c) for xl in range(NX) for y in range(NY)] for c in range(NC)]


def core_swap():
    return [(i, i ^ 1) for i in range(NX * NY * NC)]


def x_shift(d):
    pairs = []
    for z in range(NZ):
        for x in range(XN):
            to = (x + d) % XN
            for y in range(NY):
                for c in range(NC):
                    src = (z * 2 + x // 2) * 32 + blk_of(x % 2, y, c)
                    dst = (z * 2 + to // 2) * 32 + blk_of(to % 2, y, c)
                    pairs.append((src, dst))
    return pairs


def nn(a, b):
    return lax.dot_general(a, b, (((1,), (0,)), ((), ())), preferred_element_type=F32)


def nt(a, b):
    return lax.dot_general(a, b, (((1,), (1,)), ((), ())), preferred_element_type=F32)


def iota(shape, dim):
    return lax.broadcasted_iota(jnp.int32, shape, dim)


def spread(rows, lam, lam_pad, o_store):
    total = rows.shape[1]
    width_in, width_out = 8 * lam, 8 * lam_pad
    for i in range(total // width_in):
        lo = width_in * i // 128 * 128
        off = width_in * i - lo
        hi = min(lo + (off + width_in + 127) // 128 * 128, total)
        window = rows[:, lo:hi]
        shape = (hi - lo, width_out)
        r, c = iota(shape, 0), iota(shape, 1)
        block = c // lam_pad
        within = c - block * lam_pad
        pick = (within < lam) & (r == off + block * lam + within)
        o_store(i * width_out, nn(window, jnp.where(pick, 1.0, 0.0).astype(BF)).astype(BF))


def pad_v_kernel(lam, lam_pad, v_ref, o_ref):
    def store(at, val):
        o_ref[:, at : at + val.shape[1]] = val

    spread(v_ref[...], lam, lam_pad, store)


def split_kernel(v_ref, lo_ref, hi_ref):
    blocks, width, _ = v_ref.shape
    pad = lo_ref.shape[0] // (blocks // 2)
    for n, ref in enumerate((lo_ref, hi_ref)):
        for i in range(blocks // 2):
            ref[i * pad + width // 16 * 16 : (i + 1) * pad, :] = jnp.zeros((pad - width // 16 * 16, ref.shape[1]), BF)
            ref[i * pad : i * pad + width, :] = v_ref[n * blocks // 2 + i]


def arrange_kernel(lam, lam_pad, core_ref, own_ref, oth_ref, o_ref):
    n_in = own_ref.shape[0]
    n_out = o_ref.shape[1]
    shape = (n_out, n_in)
    r, c = iota(shape, 0), iota(shape, 1)
    s = r // lam_pad
    l = r - s * lam_pad
    perm = jnp.where((l < lam) & (c == l * 8 + s), 1.0, 0.0).astype(BF)
    core = core_ref[0]
    for ref, at in ((own_ref, core), (oth_ref, 1 - core)):
        rows = nn(perm, ref[...]).astype(BF)

        def store(col, val, at=at):
            o_ref[at, :, col : col + val.shape[1]] = val

        spread(rows, lam, lam_pad, store)


def half_kernel(pad, xl_ref, a_ref, v0_ref, v1_ref, v2_ref, v3_ref, o_ref, w_ref, g_ref):
    xl = xl_ref[0]
    half = NY * pad
    for n, ref in enumerate((v0_ref, v1_ref, v2_ref, v3_ref)):
        x = xl if n < 2 else 1 - xl
        at = pl.multiple_of(x * half + n % 2 * (half // 2), half // 2)
        w_ref[pl.ds(at, half // 2), :] = ref[...]
    rows = 16
    shape = (rows, 8 * pad)
    block = iota(shape, 1) // pad
    masks = {b: (block & b) != 0 for b in (4, 2, 1)}
    for x in range(NX):
        w = w_ref[x * half : (x + 1) * half, :]
        for core in range(NC):
            g_ref[...] = nt(a_ref[core], w)
            for l0 in range(0, pad, rows):
                g = [g_ref[s * pad + l0 : s * pad + l0 + rows, :] for s in range(8)]
                for b in (4, 2, 1):
                    new = list(g)
                    for s in range(8):
                        if s & b == 0:
                            lo, hi = g[s], g[s | b]
                            new[s] = jnp.where(masks[b], pltpu.roll(hi, pad * b, 1), lo)
                            new[s | b] = jnp.where(masks[b], hi, pltpu.roll(lo, 8 * pad - pad * b, 1))
                    g = new
                for y in range(NY):
                    o_ref[x * NY + y, core * pad + l0 : core * pad + l0 + rows, :] = g[y].astype(BF)


def third_kernel(pad, where_ref, owner_ref, r_ref, *refs):
    v_refs, o_ref, w_ref, pos_ref = refs[:8], refs[8], refs[9], refs[10]
    blocks = NX * NY * NC
    for p in range(blocks):
        pos_ref[owner_ref[p]] = p
    xl, core = where_ref[0], where_ref[1]
    for n, ref in enumerate(v_refs):
        c = core if n < 4 else 1 - core
        x = xl if n % 4 < 2 else 1 - xl
        for i in range(NY // 2):
            k = (x * NY + n % 2 * (NY // 2) + i) * NC + c
            at = pl.multiple_of(pos_ref[k] * pad, pad)
            w_ref[pl.ds(at, pad), :] = ref[i * pad : (i + 1) * pad, :]
    r = r_ref[...].reshape(r_ref.shape[0] * r_ref.shape[1], r_ref.shape[2])
    per = o_ref.shape[1]
    for m in range(0, o_ref.shape[0], 4):
        out = nn(w_ref[m * per : (m + 4) * per, :], r).astype(BF)
        o_ref[m : m + 4] = out.reshape(4, per, out.shape[1])


def gather_kernel(pad, start_ref, x_ref, o_ref, t_ref):
    groups, rows_in, lanes = x_ref.shape
    n_a, n_b, _ = o_ref.shape
    shape = (n_a * 8, lanes)
    r, c = iota(shape, 0), iota(shape, 1)
    a = r // 8
    pick = jnp.where(c == (r - a * 8) * pad + a, 1.0, 0.0).astype(BF)
    fill = jnp.zeros((128 - rows_in, lanes), BF)
    for g in range(groups):
        rank = jnp.int32(0)
        for h in range(groups):
            rank = rank + (start_ref[h] < start_ref[g]).astype(jnp.int32)
        t_ref[rank] = nt(pick, jnp.concatenate([x_ref[g], fill], axis=0)).astype(BF).astype(F32)
    shape = (n_b, 128)
    r, c = iota(shape, 0), iota(shape, 1)
    half = n_b // 2
    tight = jnp.where(c == jnp.where(r < half, r, r - half + pad), 1.0, 0.0).astype(BF)
    for a in range(n_a):
        tile = t_ref[:, a * 8 : (a + 1) * 8, :].reshape(groups * 8, 128).astype(BF)
        o_ref[a] = nt(tight, tile).astype(BF)


SMEM = pl.BlockSpec(memory_space=pltpu.SMEM)
VMEM = pl.BlockSpec(memory_space=pltpu.VMEM)


def call(kernel, out_shape, n_smem, n_vmem, scratch=(), flops=0, moved=0):
    return pl.pallas_call(
        kernel,
        out_shape=jax.ShapeDtypeStruct(out_shape, BF),
        in_specs=[SMEM] * n_smem + [VMEM] * n_vmem,
        out_specs=VMEM,
        scratch_shapes=list(scratch),
        cost_estimate=pl.CostEstimate(flops=flops, bytes_accessed=moved, transcendentals=0),
    )


def local(ao_ints, v_coeff, batch_start, owner_map):
    sig, lam, nao = ao_ints.shape
    width = v_coeff.shape[1]
    pad = 48
    nblk, ngrp = owner_map.shape[0], batch_start.shape[0]
    kdim = nblk * pad
    me = lax.axis_index("blk").astype(jnp.int32)
    core, xl = me % NC, me // (NY * NC)
    ao_rows = ao_ints.transpose(1, 0, 2).reshape(lam * sig, nao)
    ao_other = lax.ppermute(ao_rows, "blk", core_swap())
    v_pad = call(functools.partial(pad_v_kernel, lam, pad), (width, kdim), 0, 1)(v_coeff.T)
    v_y = lax.all_gather(v_pad, "blk", axis=0, axis_index_groups=y_groups())
    part = jax.ShapeDtypeStruct((NY // 2 * pad, kdim), BF)
    v_y0, v_y1 = pl.pallas_call(
        split_kernel, out_shape=(part, part), in_specs=[VMEM], out_specs=(VMEM, VMEM), name="split"
    )(v_y)
    v_x0 = lax.ppermute(v_y0, ("grp", "blk"), x_shift(1))
    v_x1 = lax.ppermute(v_y1, ("grp", "blk"), x_shift(-1))
    mine = (v_y0, v_y1, v_x0, v_x1)
    ao = call(
        functools.partial(arrange_kernel, lam, pad), (NC, sig * pad, kdim), 1, 2,
        flops=6 * 10**9, moved=5 * 10**6,
    )(core.reshape(1), ao_rows, ao_other)
    halves = call(
        functools.partial(half_kernel, pad), (NX * NY, NC * pad, sig * pad), 1, 5,
        scratch=[pltpu.VMEM((NX * NY * pad, kdim), BF), pltpu.VMEM((sig * pad, NY * pad), F32)],
        flops=2 * 10**9, moved=6 * 10**6,
    )(xl.reshape(1), ao, *mine)
    owned = lax.all_to_all(halves, "blk", split_axis=0, concat_axis=0, tiled=True, axis_index_groups=xy_groups())
    swapped = [lax.ppermute(v, "blk", core_swap()) for v in mine]
    third = call(
        functools.partial(third_kernel, pad), (ngrp, nblk // ngrp * pad, sig * pad), 2, 9,
        scratch=[pltpu.VMEM((kdim, kdim), BF), pltpu.SMEM((nblk,), jnp.int32)],
        flops=2 * 10**9, moved=7 * 10**6,
    )(jnp.stack([xl, core]), owner_map, owned, *mine, *swapped)
    received = lax.all_to_all(third, "grp", split_axis=0, concat_axis=0, tiled=True)
    out = call(
        functools.partial(gather_kernel, pad), (width, nblk // ngrp * width, ngrp * sig), 1, 1,
        scratch=[pltpu.VMEM((ngrp, width * 8, 128), F32)],
        flops=10**9, moved=2 * 10**6,
    )(batch_start, received)
    return out.transpose(2, 0, 1)


def solution(mesh):
    return jax.shard_map(
        local,
        mesh=mesh,
        in_specs=(P("grp", "blk", None), P(None, "blk"), P(), P()),
        out_specs=P(None, "blk", "grp"),
        check_vma=False,
    )
```

```python
import functools

import jax
import jax.numpy as jnp
from jax import lax
from jax.experimental import pallas as pl
from jax.experimental.pallas import tpu as pltpu
from jax.sharding import PartitionSpec as P


BF = jnp.bfloat16
F32 = jnp.float32
NX, NY, NZ, NC = 2, 8, 8, 2
XN = 4


def blk_of(xl, y, c):
    return (xl * NY + y) * NC + c


def y_groups():
    return [[blk_of(xl, y, c) for y in range(NY)] for xl in range(NX) for c in range(NC)]


def xy_groups():
    return [[blk_of(xl, y, c) for xl in range(NX) for y in range(NY)] for c in range(NC)]


def core_swap():
    return [(i, i ^ 1) for i in range(NX * NY * NC)]


def x_shift(d):
    pairs = []
    for z in range(NZ):
        for x in range(XN):
            to = (x + d) % XN
            for y in range(NY):
                for c in range(NC):
                    src = (z * 2 + x // 2) * 32 + blk_of(x % 2, y, c)
                    dst = (z * 2 + to // 2) * 32 + blk_of(to % 2, y, c)
                    pairs.append((src, dst))
    return pairs


def nn(a, b):
    return lax.dot_general(a, b, (((1,), (0,)), ((), ())), preferred_element_type=F32)


def nt(a, b):
    return lax.dot_general(a, b, (((1,), (1,)), ((), ())), preferred_element_type=F32)


def iota(shape, dim):
    return lax.broadcasted_iota(jnp.int32, shape, dim)


def spread(rows, lam, lam_pad, o_store):
    total = rows.shape[1]
    width_in, width_out = 8 * lam, 8 * lam_pad
    for i in range(total // width_in):
        lo = width_in * i // 128 * 128
        off = width_in * i - lo
        hi = min(lo + (off + width_in + 127) // 128 * 128, total)
        window = rows[:, lo:hi]
        shape = (hi - lo, width_out)
        r, c = iota(shape, 0), iota(shape, 1)
        block = c // lam_pad
        within = c - block * lam_pad
        pick = (within < lam) & (r == off + block * lam + within)
        o_store(i * width_out, nn(window, jnp.where(pick, 1.0, 0.0).astype(BF)).astype(BF))


def pad_v_kernel(lam, lam_pad, v_ref, o_ref):
    width = v_ref.shape[0]
    tall = width // 8 * 8
    rest = width - tall

    def store(at, val):
        q = at // val.shape[1]
        o_ref[q * tall : (q + 1) * tall, :] = val[:tall]
        o_ref[4 * tall + q * rest : 4 * tall + (q + 1) * rest, :] = val[tall:]

    spread(v_ref[...], lam, lam_pad, store)


def split(ref0, ref1, width):
    first = width // 8 * 16
    return ((ref0, first, 0), (ref1, 4 * width - first, 0))


def unstack(parts, i, width, w_ref, at, zeros_to=0):
    tall = width // 8 * 8
    rest = width - tall
    (ref0, step0, low), (ref1, step1, high) = parts
    low, high, quarter = low + i * step0, high + i * step1, ref0.shape[1]
    if zeros_to:
        w_ref[pl.ds(at + tall, zeros_to - tall), :] = jnp.zeros((zeros_to - tall, w_ref.shape[1]), BF)
    for q in range(4):
        lanes = slice(q * quarter, (q + 1) * quarter)
        ref, row = (ref0, low + q * tall) if q < 2 else (ref1, high + (q - 2) * tall)
        w_ref[pl.ds(at, tall), lanes] = ref[row : row + tall, :]
        row = high + 2 * tall + q * rest
        w_ref[pl.ds(at + tall, rest), lanes] = ref1[row : row + rest, :]


def arrange_kernel(lam, lam_pad, ao_ref, o_ref):
    shape = (o_ref.shape[0], ao_ref.shape[0])
    r, c = iota(shape, 0), iota(shape, 1)
    s = r // lam_pad
    l = r - s * lam_pad
    perm = jnp.where((l < lam) & (c == l * 8 + s), 1.0, 0.0).astype(BF)

    def store(col, val):
        o_ref[:, col : col + val.shape[1]] = val

    spread(nn(perm, ao_ref[...]).astype(BF), lam, lam_pad, store)


def half_column(pad, width, core, a_refs, w_ref, g_ref, store, done=None):
    rows = 16
    lane = iota((rows, 128), 1)
    for n, a_ref in enumerate(a_refs):
        g_ref[core if n == 0 else 1 - core] = nt(a_ref[...], w_ref[...])
    per = pad // rows
    chunks = NC * per

    def place(y, s, n, column):
        lo, off = pad * y % 128, column * width
        top = s * pad + n % per * rows
        tile = pad * y // 128 * 128

        def turned(x):
            return pltpu.roll(x, (off - lo) % 128, 1) if (off - lo) % 128 else x

        out = turned(g_ref[n // per, top : top + rows, tile : tile + 128])
        if lo + width > 128:
            out = jnp.where(lane < off + 128 - lo, out, turned(g_ref[n // per, top : top + rows, tile + 128 : tile + 256]))
        return out

    def emit(y, row, cells):
        out = place(y, *cells[2], 2)
        out = jnp.where(lane < 2 * width, place(y, *cells[1], 1), out)
        out = jnp.where(lane < width, place(y, *cells[0], 0), out)
        store(y, row, out.astype(BF))

    third = 2 * chunks // 3
    last = [(6 + i // chunks, i % chunks) for i in range(2 * chunks)]
    for y in range(NY):
        for group in range(2):
            for n in range(chunks):
                emit(y, (group * chunks + n) * rows, [(3 * group + i, n) for i in range(3)])
        for n in range(third):
            emit(y, (2 * chunks + n) * rows, [last[i * third + n] for i in range(3)])
        if done is not None and y % 2:
            done(y - 1)


def half_own_kernel(pad, width, where_ref, a0_ref, a1_ref, v0_ref, v1_ref, o_ref, w_ref, g_ref):
    for i in range(NY):
        unstack(split(v0_ref, v1_ref, width), i, width, w_ref, i * pad, pad)

    def store(y, row, val):
        o_ref[y, row : row + val.shape[0], :] = val

    half_column(pad, width, where_ref[1], (a0_ref, a1_ref), w_ref, g_ref, store)


def half_other_kernel(
    pad, width, where_ref, a0_ref, a1_ref, v0_ref, v1_ref, own_ref, o_ref, w_ref, g_ref, b_ref, sems
):
    xl = where_ref[0]
    first = (1 - xl) * NY
    own = pltpu.make_async_copy(own_ref, o_ref.at[pl.ds(xl * NY, NY)], sems.at[NY // 2])
    own.start()
    for i in range(NY):
        unstack(split(v0_ref, v1_ref, width), i, width, w_ref, i * pad, pad)
    copies = []

    def store(y, row, val):
        b_ref[y, row : row + val.shape[0], :] = val

    def done(y):
        copies.append(pltpu.make_async_copy(b_ref.at[pl.ds(y, 2)], o_ref.at[pl.ds(first + y, 2)], sems.at[y // 2]))
        copies[-1].start()

    half_column(pad, width, where_ref[1], (a0_ref, a1_ref), w_ref, g_ref, store, done)
    own.wait()
    for copy in copies:
        copy.wait()


def third_kernel(pad, width, where_ref, owner_ref, r_ref, *refs):
    o_ref, w_ref, rt_ref, g_ref, pos_ref, sems, s_ref = refs[4:]
    blocks = NX * NY * NC
    for p in range(blocks):
        pos_ref[owner_ref[p]] = p
    xl, core = where_ref[0], where_ref[1]
    for n in range(4):
        c = core if n < 2 else 1 - core
        x = xl if n % 2 == 0 else 1 - xl
        for i in range(NY):
            p = pos_ref[(x * NY + i) * NC + c]
            at = pl.multiple_of((p >> 1) * 128 + (p & 1) * pad, 16)
            part = refs[n].at[pl.ds(i * pad, pad), :]
            pltpu.make_async_copy(part, w_ref.at[pl.ds(at, pad), :], sems.at[p]).start()
    high = NC * pad
    low = r_ref.shape[1] - 2 * high
    lane = iota((low // 2, 128), 1)
    for i in range(r_ref.shape[0]):
        top = i * high
        s_ref[top : top + high, :128] = r_ref[i, :high]
        s_ref[top : top + high, 128:256] = r_ref[i, high : 2 * high]
        up, down = (r_ref[i, 2 * high + n * low // 2 : 2 * high + (n + 1) * low // 2].astype(F32) for n in range(2))
        up_left, down_left = (pltpu.roll(x, 128 - width, 1) for x in (up, down))
        cells = ((up, down), (down, up_left), (up_left, down_left))
        for n, (six, seven) in enumerate(cells):
            at = top + n * (low // 2)
            s_ref[at : at + low // 2, 256:] = jnp.where(lane < width, six, seven).astype(BF)
    shape = (rt_ref.shape[0], s_ref.shape[1])
    r, c = iota(shape, 0), iota(shape, 1)
    a = r // 8
    s = r - a * 8
    group = s // 3
    pick = jnp.where(c == group * 128 + (s - group * 3) * width + a, 1.0, 0.0).astype(BF)
    rt_ref[...] = nt(pick, s_ref[...]).astype(BF)
    third = rt_ref.shape[0] // 3
    rows = 16
    lane = iota((rows, 128), 1)
    for m in range(0, o_ref.shape[0], 2):
        at = m // 2 % 2
        for p in range(2 * m, 2 * m + 4):
            here = w_ref.at[pl.ds(p // 2 * 128 + p % 2 * pad, pad), :]
            pltpu.make_async_copy(refs[0].at[pl.ds(0, pad), :], here, sems.at[p]).wait()
        g_ref[at] = nt(rt_ref[...], w_ref[m * 128 : (m + 2) * 128, :])
        for d in range(2):
            for r0 in range(0, third, rows):
                g = [g_ref[at, n * third + r0 : n * third + r0 + rows, d * 128 : (d + 1) * 128] for n in range(3)]
                for p in range(2):
                    turned = [pltpu.roll(x, (n * width - p * pad) % 128, 1) if n or p else x for n, x in enumerate(g)]
                    out = jnp.where(lane < 3 * width, turned[2], 0.0)
                    out = jnp.where(lane < 2 * width, turned[1], out)
                    out = jnp.where(lane < width, turned[0], out)
                    o_ref[m + d, p * third + r0 : p * third + r0 + rows, :] = out.astype(BF)


def gather_kernel(start_ref, x_ref, o_ref, t_ref):
    groups = x_ref.shape[0]
    n_a, n_b, _ = o_ref.shape
    for g in range(groups):
        rank = jnp.int32(0)
        for h in range(groups):
            rank = rank + (start_ref[h] < start_ref[g]).astype(jnp.int32)
        t_ref[:, rank] = x_ref[g].reshape(t_ref.shape[0], 8, 128)
    eye = jnp.where(iota((128, 128), 0) == iota((128, 128), 1), 1.0, 0.0).astype(BF)
    width = n_b // 2
    for j in range(0, t_ref.shape[0], 2):
        both = nt(eye, t_ref[j : j + 2].reshape(2 * groups * 8, 128)).astype(BF)
        for i in range(2):
            p, a = divmod(j + i, n_a // 3)
            for n in range(3):
                o_ref[n * (n_a // 3) + a, p * width : (p + 1) * width, :] = both[
                    n * width : (n + 1) * width, i * 128 : (i + 1) * 128
                ]


SMEM = pl.BlockSpec(memory_space=pltpu.SMEM)
VMEM = pl.BlockSpec(memory_space=pltpu.VMEM)
HBM = pl.BlockSpec(memory_space=pltpu.HBM)


def call(kernel, out_shapes, n_smem, n_vmem, scratch=(), flops=0, moved=0, mib=12, in_hbm=0, out_hbm=False):
    outs = tuple(jax.ShapeDtypeStruct(shape, BF) for shape in out_shapes)
    res = pl.pallas_call(
        kernel,
        out_shape=outs,
        in_specs=[SMEM] * n_smem + [VMEM] * (n_vmem - in_hbm) + [HBM] * in_hbm,
        out_specs=((HBM if out_hbm else VMEM), *(VMEM,) * (len(outs) - 1)),
        scratch_shapes=list(scratch),
        compiler_params=pltpu.CompilerParams(vmem_limit_bytes=mib * 2**20),
        cost_estimate=pl.CostEstimate(flops=flops, bytes_accessed=moved, transcendentals=0),
    )
    return res


def local(ao_ints, v_coeff, batch_start, owner_map):
    sig, lam, nao = ao_ints.shape
    width = v_coeff.shape[1]
    pad = 48
    nblk, ngrp = owner_map.shape[0], batch_start.shape[0]
    kdim = nblk * pad
    me = lax.axis_index("blk").astype(jnp.int32)
    where = jnp.stack([me >> 4, me & (NC - 1)])
    ao_rows = ao_ints.transpose(1, 0, 2).reshape(lam * sig, nao)
    ao_other = lax.ppermute(ao_rows, "blk", core_swap())
    tall = width // 8 * 8
    (v_pad,) = call(functools.partial(pad_v_kernel, lam, pad), [(4 * width, kdim // 4)], 0, 1)(v_coeff.T)
    v_all = lax.all_gather(v_pad, "blk", axis=0, axis_index_groups=y_groups())
    sides = [v.reshape(-1, kdim // 4) for v in (v_all[:, : 2 * tall], v_all[:, 2 * tall :])]
    v_x = [lax.ppermute(v, ("grp", "blk"), x_shift(d)) for v, d in zip(sides, (1, -1))]
    arranged = [
        call(
            functools.partial(arrange_kernel, lam, pad), [(sig * pad, kdim)], 0, 1,
            flops=3 * 10**9, moved=2 * 10**6,
        )(rows)[0]
        for rows in (ao_rows, ao_other)
    ]
    rows = NC * pad * sig // 3
    scratch = [pltpu.VMEM((NC, sig * pad, NY * pad), F32)]
    own, w_own = call(
        functools.partial(half_own_kernel, pad, width), [(NY, rows, 128), (NY * pad, kdim)], 1, 4,
        scratch=scratch, flops=2 * 10**9, moved=3 * 10**6,
    )(where, *arranged, *sides)
    halves, w_other = call(
        functools.partial(half_other_kernel, pad, width), [(NX * NY, rows, 128), (NY * pad, kdim)], 1, 5,
        scratch=scratch + [pltpu.VMEM((NY, rows, 128), BF), pltpu.SemaphoreType.DMA((NY // 2 + 1,))],
        flops=2 * 10**9, moved=3 * 10**6, out_hbm=True,
    )(where, *arranged, *v_x, own)
    owned = lax.all_to_all(halves, "blk", split_axis=0, concat_axis=0, tiled=True, axis_index_groups=xy_groups())
    mine = (w_own, w_other)
    swapped = [lax.ppermute(w, "blk", core_swap()) for w in mine]
    afar = [pltpu.with_memory_space_constraint(w, pltpu.HBM) for w in (*mine, *swapped)]
    (third,) = call(
        functools.partial(third_kernel, pad, width), [(ngrp, width * sig * 2 // 3, 128)], 2, 5,
        scratch=[
            pltpu.VMEM((ngrp * 128, kdim), BF), pltpu.VMEM((width * sig, kdim), BF),
            pltpu.VMEM((2, width * sig, 256), F32), pltpu.SMEM((nblk,), jnp.int32),
            pltpu.SemaphoreType.DMA((nblk,)),
            pltpu.VMEM((kdim, 384), BF),
        ],
        flops=2 * 10**9, moved=7 * 10**6, mib=20, in_hbm=4,
    )(where, owner_map, owned, *afar)
    received = lax.all_to_all(third, "grp", split_axis=0, concat_axis=0, tiled=True)
    (out,) = call(
        gather_kernel, [(width, nblk // ngrp * width, ngrp * sig)], 1, 1,
        scratch=[pltpu.VMEM((width * 2 // 3, ngrp, sig, 128), BF)],
        flops=10**9, moved=2 * 10**6,
    )(batch_start, received)
    return out.transpose(2, 0, 1)


def solution(mesh):
    return jax.shard_map(
        local,
        mesh=mesh,
        in_specs=(P("grp", "blk", None), P(None, "blk"), P(), P()),
        out_specs=P(None, "blk", "grp"),
        check_vma=False,
    )
```

```python
import functools

import jax
import jax.numpy as jnp
from jax import lax
from jax.experimental import pallas as pl
from jax.experimental.pallas import tpu as pltpu
from jax.sharding import PartitionSpec as P


BF = jnp.bfloat16
F32 = jnp.float32
NX, NY, NZ, NC = 2, 8, 8, 2
XN = 4


def blk_of(xl, y, c):
    return (xl * NY + y) * NC + c


def y_groups():
    return [[blk_of(xl, y, c) for y in range(NY)] for xl in range(NX) for c in range(NC)]


def xy_groups():
    return [[blk_of(xl, y, c) for xl in range(NX) for y in range(NY)] for c in range(NC)]


def core_swap():
    return [(i, i ^ 1) for i in range(NX * NY * NC)]


def x_shift(d):
    pairs = []
    for z in range(NZ):
        for x in range(XN):
            to = (x + d) % XN
            for y in range(NY):
                for c in range(NC):
                    src = (z * 2 + x // 2) * 32 + blk_of(x % 2, y, c)
                    dst = (z * 2 + to // 2) * 32 + blk_of(to % 2, y, c)
                    pairs.append((src, dst))
    return pairs


def nn(a, b):
    return lax.dot_general(a, b, (((1,), (0,)), ((), ())), preferred_element_type=F32)


def nt(a, b):
    return lax.dot_general(a, b, (((1,), (1,)), ((), ())), preferred_element_type=F32)


def iota(shape, dim):
    return lax.broadcasted_iota(jnp.int32, shape, dim)


def spread(rows, lam, lam_pad, o_store):
    total = rows.shape[1]
    width_in, width_out = 8 * lam, 8 * lam_pad
    for i in range(total // width_in):
        lo = width_in * i // 128 * 128
        off = width_in * i - lo
        hi = min(lo + (off + width_in + 127) // 128 * 128, total)
        window = rows[:, lo:hi]
        shape = (hi - lo, width_out)
        r, c = iota(shape, 0), iota(shape, 1)
        block = c // lam_pad
        within = c - block * lam_pad
        pick = (within < lam) & (r == off + block * lam + within)
        o_store(i * width_out, nn(window, jnp.where(pick, 1.0, 0.0).astype(BF)).astype(BF))


def pad_v_kernel(lam, lam_pad, v_ref, o_ref):
    width = v_ref.shape[0]
    tall = width // 8 * 8
    rest = width - tall

    def store(at, val):
        q = at // val.shape[1]
        o_ref[q * tall : (q + 1) * tall, :] = val[:tall]
        o_ref[4 * tall + q * rest : 4 * tall + (q + 1) * rest, :] = val[tall:]

    spread(v_ref[...], lam, lam_pad, store)


def split(ref0, ref1, width):
    first = width // 8 * 16
    return ((ref0, first, 0), (ref1, 4 * width - first, 0))


def unstack(parts, i, width, w_ref, at, zeros_to=0):
    tall = width // 8 * 8
    rest = width - tall
    (ref0, step0, low), (ref1, step1, high) = parts
    low, high, quarter = low + i * step0, high + i * step1, ref0.shape[1]
    if zeros_to:
        w_ref[pl.ds(at + tall, zeros_to - tall), :] = jnp.zeros((zeros_to - tall, w_ref.shape[1]), BF)
    for q in range(4):
        lanes = slice(q * quarter, (q + 1) * quarter)
        ref, row = (ref0, low + q * tall) if q < 2 else (ref1, high + (q - 2) * tall)
        w_ref[pl.ds(at, tall), lanes] = ref[row : row + tall, :]
        row = high + 2 * tall + q * rest
        w_ref[pl.ds(at + tall, rest), lanes] = ref1[row : row + rest, :]


def arrange_kernel(lam, lam_pad, ao_ref, o_ref):
    shape = (o_ref.shape[0], ao_ref.shape[0])
    r, c = iota(shape, 0), iota(shape, 1)
    s = r // lam_pad
    l = r - s * lam_pad
    perm = jnp.where((l < lam) & (c == l * 8 + s), 1.0, 0.0).astype(BF)

    def store(col, val):
        o_ref[:, col : col + val.shape[1]] = val

    spread(nn(perm, ao_ref[...]).astype(BF), lam, lam_pad, store)


def half_column(pad, width, core, a_refs, w_ref, g_ref, store, done=None):
    rows = 16
    lane = iota((rows, 128), 1)
    for n, a_ref in enumerate(a_refs):
        g_ref[core if n == 0 else 1 - core] = nt(a_ref[...], w_ref[...])
    per = pad // rows
    chunks = NC * per

    def place(y, s, n, column):
        lo, off = pad * y % 128, column * width
        top = s * pad + n % per * rows
        tile = pad * y // 128 * 128

        def turned(x):
            return pltpu.roll(x, (off - lo) % 128, 1) if (off - lo) % 128 else x

        out = turned(g_ref[n // per, top : top + rows, tile : tile + 128])
        if lo + width > 128:
            out = jnp.where(lane < off + 128 - lo, out, turned(g_ref[n // per, top : top + rows, tile + 128 : tile + 256]))
        return out

    def emit(y, row, cells):
        out = place(y, *cells[2], 2)
        out = jnp.where(lane < 2 * width, place(y, *cells[1], 1), out)
        out = jnp.where(lane < width, place(y, *cells[0], 0), out)
        store(y, row, out.astype(BF))

    third = 2 * chunks // 3
    last = [(6 + i // chunks, i % chunks) for i in range(2 * chunks)]
    for y in range(NY):
        for group in range(2):
            for n in range(chunks):
                emit(y, (group * chunks + n) * rows, [(3 * group + i, n) for i in range(3)])
        for n in range(third):
            emit(y, (2 * chunks + n) * rows, [last[i * third + n] for i in range(3)])
        if done is not None and y % 2:
            done(y - 1)


def half_own_kernel(pad, width, where_ref, a0_ref, a1_ref, v0_ref, v1_ref, o_ref, w_ref, g_ref):
    for i in range(NY):
        unstack(split(v0_ref, v1_ref, width), i, width, w_ref, i * pad, pad)

    def store(y, row, val):
        o_ref[y, row : row + val.shape[0], :] = val

    half_column(pad, width, where_ref[1], (a0_ref, a1_ref), w_ref, g_ref, store)


def half_other_kernel(
    pad, width, where_ref, a0_ref, a1_ref, v0_ref, v1_ref, own_ref, o_ref, w_ref, g_ref, b_ref, sems
):
    xl = where_ref[0]
    first = (1 - xl) * NY
    own = pltpu.make_async_copy(own_ref, o_ref.at[pl.ds(xl * NY, NY)], sems.at[NY // 2])
    own.start()
    for i in range(NY):
        unstack(split(v0_ref, v1_ref, width), i, width, w_ref, i * pad, pad)
    copies = []

    def store(y, row, val):
        b_ref[y, row : row + val.shape[0], :] = val

    def done(y):
        copies.append(pltpu.make_async_copy(b_ref.at[pl.ds(y, 2)], o_ref.at[pl.ds(first + y, 2)], sems.at[y // 2]))
        copies[-1].start()

    half_column(pad, width, where_ref[1], (a0_ref, a1_ref), w_ref, g_ref, store, done)
    own.wait()
    for copy in copies:
        copy.wait()


def third_kernel(pad, width, where_ref, owner_ref, r_ref, *refs):
    o_ref, all_ref, w_ref, rt_ref, g_ref, sems, s_ref = refs[4:]
    size = NY * pad
    copies = [pltpu.make_async_copy(refs[n], all_ref.at[pl.ds(n * size, size), :], sems.at[n]) for n in range(4)]
    for copy in copies:
        copy.start()
    xl, core = where_ref[0], where_ref[1]
    high = NC * pad
    low = r_ref.shape[1] - 2 * high
    lane = iota((low // 2, 128), 1)
    for i in range(r_ref.shape[0]):
        top = i * high
        s_ref[top : top + high, :128] = r_ref[i, :high]
        s_ref[top : top + high, 128:256] = r_ref[i, high : 2 * high]
        up, down = (r_ref[i, 2 * high + n * low // 2 : 2 * high + (n + 1) * low // 2].astype(F32) for n in range(2))
        up_left, down_left = (pltpu.roll(x, 128 - width, 1) for x in (up, down))
        cells = ((up, down), (down, up_left), (up_left, down_left))
        for n, (six, seven) in enumerate(cells):
            at = top + n * (low // 2)
            s_ref[at : at + low // 2, 256:] = jnp.where(lane < width, six, seven).astype(BF)
    shape = (rt_ref.shape[0], s_ref.shape[1])
    r, c = iota(shape, 0), iota(shape, 1)
    a = r // 8
    s = r - a * 8
    group = s // 3
    pick = jnp.where(c == group * 128 + (s - group * 3) * width + a, 1.0, 0.0).astype(BF)
    rt_ref[...] = nt(pick, s_ref[...]).astype(BF)
    third = rt_ref.shape[0] // 3
    rows = 16
    lane = iota((rows, 128), 1)
    for copy in copies:
        copy.wait()
    for m in range(0, o_ref.shape[0], 2):
        at = m // 2 % 2
        for p in range(4):
            k = owner_ref[2 * m + p]
            n = jnp.abs((k & 1) - core) * 2 + jnp.abs((k >> 4) - xl)
            row = pl.multiple_of((n * NY + ((k >> 1) & (NY - 1))) * pad, pad)
            here = p // 2 * 128 + p % 2 * pad
            w_ref[at, here : here + pad, :] = all_ref[pl.ds(row, pad), :]
        g_ref[at] = nt(rt_ref[...], w_ref[at])
        for d in range(2):
            for r0 in range(0, third, rows):
                g = [g_ref[at, n * third + r0 : n * third + r0 + rows, d * 128 : (d + 1) * 128] for n in range(3)]
                for p in range(2):
                    turned = [pltpu.roll(x, (n * width - p * pad) % 128, 1) if n or p else x for n, x in enumerate(g)]
                    out = jnp.where(lane < 3 * width, turned[2], 0.0)
                    out = jnp.where(lane < 2 * width, turned[1], out)
                    out = jnp.where(lane < width, turned[0], out)
                    o_ref[m + d, p * third + r0 : p * third + r0 + rows, :] = out.astype(BF)


def gather_kernel(start_ref, x_ref, o_ref, t_ref):
    groups = x_ref.shape[0]
    n_a, n_b, _ = o_ref.shape
    for g in range(groups):
        rank = jnp.int32(0)
        for h in range(groups):
            rank = rank + (start_ref[h] < start_ref[g]).astype(jnp.int32)
        t_ref[:, rank] = x_ref[g].reshape(t_ref.shape[0], 8, 128)
    eye = jnp.where(iota((128, 128), 0) == iota((128, 128), 1), 1.0, 0.0).astype(BF)
    width = n_b // 2
    for j in range(0, t_ref.shape[0], 2):
        both = nt(eye, t_ref[j : j + 2].reshape(2 * groups * 8, 128)).astype(BF)
        for i in range(2):
            p, a = divmod(j + i, n_a // 3)
            for n in range(3):
                o_ref[n * (n_a // 3) + a, p * width : (p + 1) * width, :] = both[
                    n * width : (n + 1) * width, i * 128 : (i + 1) * 128
                ]


SMEM = pl.BlockSpec(memory_space=pltpu.SMEM)
VMEM = pl.BlockSpec(memory_space=pltpu.VMEM)
HBM = pl.BlockSpec(memory_space=pltpu.HBM)


def call(kernel, out_shapes, n_smem, n_vmem, scratch=(), flops=0, moved=0, mib=12, in_hbm=0, out_hbm=False):
    outs = tuple(jax.ShapeDtypeStruct(shape, BF) for shape in out_shapes)
    res = pl.pallas_call(
        kernel,
        out_shape=outs,
        in_specs=[SMEM] * n_smem + [VMEM] * (n_vmem - in_hbm) + [HBM] * in_hbm,
        out_specs=((HBM if out_hbm else VMEM), *(VMEM,) * (len(outs) - 1)),
        scratch_shapes=list(scratch),
        compiler_params=pltpu.CompilerParams(vmem_limit_bytes=mib * 2**20),
        cost_estimate=pl.CostEstimate(flops=flops, bytes_accessed=moved, transcendentals=0),
    )
    return res


def local(ao_ints, v_coeff, batch_start, owner_map):
    sig, lam, nao = ao_ints.shape
    width = v_coeff.shape[1]
    pad = 48
    nblk, ngrp = owner_map.shape[0], batch_start.shape[0]
    kdim = nblk * pad
    me = lax.axis_index("blk").astype(jnp.int32)
    where = jnp.stack([me >> 4, me & (NC - 1)])
    ao_rows = ao_ints.transpose(1, 0, 2).reshape(lam * sig, nao)
    ao_other = lax.ppermute(ao_rows, "blk", core_swap())
    tall = width // 8 * 8
    (v_pad,) = call(functools.partial(pad_v_kernel, lam, pad), [(4 * width, kdim // 4)], 0, 1)(v_coeff.T)
    v_all = lax.all_gather(v_pad, "blk", axis=0, axis_index_groups=y_groups())
    sides = [v.reshape(-1, kdim // 4) for v in (v_all[:, : 2 * tall], v_all[:, 2 * tall :])]
    v_x = [lax.ppermute(v, ("grp", "blk"), x_shift(d)) for v, d in zip(sides, (1, -1))]
    arranged = [
        call(
            functools.partial(arrange_kernel, lam, pad), [(sig * pad, kdim)], 0, 1,
            flops=3 * 10**9, moved=2 * 10**6,
        )(rows)[0]
        for rows in (ao_rows, ao_other)
    ]
    rows = NC * pad * sig // 3
    scratch = [pltpu.VMEM((NC, sig * pad, NY * pad), F32)]
    own, w_own = call(
        functools.partial(half_own_kernel, pad, width), [(NY, rows, 128), (NY * pad, kdim)], 1, 4,
        scratch=scratch, flops=2 * 10**9, moved=3 * 10**6,
    )(where, *arranged, *sides)
    halves, w_other = call(
        functools.partial(half_other_kernel, pad, width), [(NX * NY, rows, 128), (NY * pad, kdim)], 1, 5,
        scratch=scratch + [pltpu.VMEM((NY, rows, 128), BF), pltpu.SemaphoreType.DMA((NY // 2 + 1,))],
        flops=2 * 10**9, moved=3 * 10**6, out_hbm=True,
    )(where, *arranged, *v_x, own)
    owned = lax.all_to_all(halves, "blk", split_axis=0, concat_axis=0, tiled=True, axis_index_groups=xy_groups())
    mine = (w_own, w_other)
    swapped = [lax.ppermute(w, "blk", core_swap()) for w in mine]
    afar = [*mine, *(pltpu.with_memory_space_constraint(w, pltpu.HBM) for w in swapped)]
    (third,) = call(
        functools.partial(third_kernel, pad, width), [(ngrp, width * sig * 2 // 3, 128)], 2, 5,
        scratch=[
            pltpu.VMEM((kdim, kdim), BF), pltpu.VMEM((2, 256, kdim), BF), pltpu.VMEM((width * sig, kdim), BF),
            pltpu.VMEM((2, width * sig, 256), F32), pltpu.SemaphoreType.DMA((4,)), pltpu.VMEM((kdim, 384), BF),
        ],
        flops=2 * 10**9, moved=7 * 10**6, mib=20, in_hbm=2,
    )(where, owner_map, owned, *afar)
    received = lax.all_to_all(third, "grp", split_axis=0, concat_axis=0, tiled=True)
    (out,) = call(
        gather_kernel, [(width, nblk // ngrp * width, ngrp * sig)], 1, 1,
        scratch=[pltpu.VMEM((width * 2 // 3, ngrp, sig, 128), BF)],
        flops=10**9, moved=2 * 10**6,
    )(batch_start, received)
    return out.transpose(2, 0, 1)


def solution(mesh):
    return jax.shard_map(
        local,
        mesh=mesh,
        in_specs=(P("grp", "blk", None), P(None, "blk"), P(), P()),
        out_specs=P(None, "blk", "grp"),
        check_vma=False,
    )
```
